32 devices in a mesh: gx: 2 (over y), gy: 16 (over z, x, core).
Axes of the slice: x: 2, y: 2, z: 4, core: 2. Of those that a mesh axis runs over, the one named last changes fastest.
Arguments:
- enc_input: bfloat16 [4096, 768], P('gy', 'gx'), may hold values from -6 to 6
- dec_input: bfloat16 [4096, 768], P('gy', 'gx'), may hold values from -6 to 6
- doc_ids: int32 [4, 1024], replicated, may hold values from 0 to 3, never falling along the last dimension, each value on 1 to 512 neighbouring positions
- block_ids: int32 [4, 1024], replicated, may hold values from 0 to 7, never falling along the last dimension, each value on 1 to 256 neighbouring positions
- enc_qkv_weight: bfloat16 [3, 768, 768], P(None, 'gx', 'gy'), may hold values from -0.21875 to 0.21875
- enc_qv_bias: bfloat16 [2, 768], P(None, 'gx'), may hold values from -1.5 to 1.5
- enc_out_weight: bfloat16 [768, 768], P('gx', 'gy'), may hold values from -1.75 to 1.75
- enc_out_bias: bfloat16 [768], P('gx'), may hold values from -1.5 to 1.5
- enc_up_weight: bfloat16 [768, 3072], P('gx', 'gy'), may hold values from -0.21875 to 0.21875
- enc_up_bias: bfloat16 [3072], P('gy'), may hold values from -1.5 to 1.5
- enc_down_weight: bfloat16 [3072, 768], P('gy', 'gx'), may hold values from -0.109375 to 0.109375
- enc_down_bias: bfloat16 [768], P('gx'), may hold values from -1.5 to 1.5
- enc_norm_gain: bfloat16 [2, 768], P(None, 'gx'), may hold values from 0.5 to 1.5
- enc_norm_bias: bfloat16 [2, 768], P(None, 'gx'), may hold values from -1.5 to 1.5
- self_qkv_weight: bfloat16 [3, 768, 768], P(None, 'gx', 'gy'), may hold values from -0.21875 to 0.21875
- self_qv_bias: bfloat16 [2, 768], P(None, 'gx'), may hold values from -1.5 to 1.5
- self_out_weight: bfloat16 [768, 768], P('gx', 'gy'), may hold values from -1.75 to 1.75
- self_out_bias: bfloat16 [768], P('gx'), may hold values from -1.5 to 1.5
- cross_qkv_weight: bfloat16 [3, 768, 768], P(None, 'gx', 'gy'), may hold values from -0.21875 to 0.21875
- cross_qv_bias: bfloat16 [2, 768], P(None, 'gx'), may hold values from -1.5 to 1.5
- cross_out_weight: bfloat16 [768, 768], P('gx', 'gy'), may hold values from -1.75 to 1.75
- cross_out_bias: bfloat16 [768], P('gx'), may hold values from -1.5 to 1.5
- dec_up_weight: bfloat16 [768, 3072], P('gx', 'gy'), may hold values from -0.21875 to 0.21875
- dec_up_bias: bfloat16 [3072], P('gy'), may hold values from -1.5 to 1.5
- dec_down_weight: bfloat16 [3072, 768], P('gy', 'gx'), may hold values from -0.109375 to 0.109375
- dec_down_bias: bfloat16 [768], P('gx'), may hold values from -1.5 to 1.5
- dec_norm_gain: bfloat16 [3, 768], P(None, 'gx'), may hold values from 0.5 to 1.5
- dec_norm_bias: bfloat16 [3, 768], P(None, 'gx'), may hold values from -1.5 to 1.5
- enc_cotangent: bfloat16 [4096, 768], P('gy', 'gx'), may hold values from -6 to 6
- dec_cotangent: bfloat16 [4096, 768], P('gy', 'gx'), may hold values from -6 to 6
Outputs:
- enc_output: bfloat16 [4096, 768], P('gy', 'gx')
- dec_output: bfloat16 [4096, 768], P('gy', 'gx')
- enc_input_grad: float32 [4096, 768], P('gy', 'gx')
- dec_input_grad: float32 [4096, 768], P('gy', 'gx')
- grad_enc_qkv_weight: float32 [3, 768, 768], P(None, 'gx', 'gy')
- grad_enc_qv_bias: float32 [2, 768], P(None, 'gx')
- grad_enc_out_weight: float32 [768, 768], P('gx', 'gy')
- grad_enc_out_bias: float32 [768], P('gx')
- grad_enc_up_weight: float32 [768, 3072], P('gx', 'gy')
- grad_enc_up_bias: float32 [3072], P('gy')
- grad_enc_down_weight: float32 [3072, 768], P('gy', 'gx')
- grad_enc_down_bias: float32 [768], P('gx')
- grad_enc_norm_gain: float32 [2, 768], P(None, 'gx')
- grad_enc_norm_bias: float32 [2, 768], P(None, 'gx')
- grad_self_qkv_weight: float32 [3, 768, 768], P(None, 'gx', 'gy')
- grad_self_qv_bias: float32 [2, 768], P(None, 'gx')
- grad_self_out_weight: float32 [768, 768], P('gx', 'gy')
- grad_self_out_bias: float32 [768], P('gx')
- grad_cross_qkv_weight: float32 [3, 768, 768], P(None, 'gx', 'gy')
- grad_cross_qv_bias: float32 [2, 768], P(None, 'gx')
- grad_cross_out_weight: float32 [768, 768], P('gx', 'gy')
- grad_cross_out_bias: float32 [768], P('gx')
- grad_dec_up_weight: float32 [768, 3072], P('gx', 'gy')
- grad_dec_up_bias: float32 [3072], P('gy')
- grad_dec_down_weight: float32 [3072, 768], P('gy', 'gx')
- grad_dec_down_bias: float32 [768], P('gx')
- grad_dec_norm_gain: float32 [3, 768], P(None, 'gx')
- grad_dec_norm_bias: float32 [3, 768], P(None, 'gx')
The draws below stay inside these ranges and needn't reach their ends.
Inputs may be any that keep to these rules, and one draw needn't show every extreme that they name: `doc_ids`: each row holds one sequence's document ids: they never fall along the row, start at 0, every id is used, each document has 1 to 512 positions and one has exactly 512. `block_ids`: each row holds one sequence's block index per position: never falling, starting at 0, every index used, each block 1 to 256 positions and one exactly 256.
All inputs are finite; a program needn't handle non-finite values.
Results may differ from the reference program's by a relative error of at most 0.022.
Values may be sent and summed in bfloat16 or wider, within the bound.
No kernel may reach another device: no remote copies, remote signals or barrier semaphores. Data moves between devices by JAX's collectives and lax.ppermute only.
A program may use at most 192 MiB of HBM per device.

```python
import math
import jax
import jax.numpy as jnp
import numpy as np
from jax import lax

D = 768
HEADS = 12
HEAD_DIM = 64
FF = 3072
BLOCK = 256
DOCS = 4
SEQ = 1024
NBLOCKS = 8
TOKENS = 4096
SEQS = 4


def spiked(entries, key, source, target, parts, factor):
    def block_of(dim):
        return (jnp.arange(entries.shape[dim]) // (entries.shape[dim] // parts)).reshape((-1,) + (1,) * (entries.ndim - 1 - dim))

    first = jax.random.permutation(key, parts)[block_of(target)]
    other_side = (block_of(target) + parts // 2) % parts
    return jnp.where((block_of(source) == first) | (block_of(source) == other_side), factor * entries, entries)


def levels(key, shape, shards, least, top_value):
    level = 1.0
    for position, shards_of in shards:
        heights = jax.random.uniform(jax.random.fold_in(jax.random.fold_in(key, 6), position), (shards_of,), jnp.float32, least / len(shards), top_value / len(shards))
        level = level * jnp.repeat(jnp.exp(heights), shape[position] // shards_of).reshape((-1,) + (1,) * (len(shape) - 1 - position))
    return level


def length_profile(amount, total, bound, skew):
    portions = [(1 << 20) // math.isqrt(grade ** skew) + 1 for grade in range(2, amount + 1)]
    surplus, counts = total - bound - (amount - 1), [1] * (amount - 1)
    while surplus > 0:
        free = [i for i in range(amount - 1) if counts[i] < bound]
        pool, left = sum([portions[i] for i in free]), surplus
        for i in free:
            addition = min(bound - counts[i], max(1, left * portions[i] // pool), surplus)
            counts[i] = counts[i] + addition
            surplus = surplus - addition
    return np.array([bound] + counts)


def ragged_sizes(stream_key, count, total, bound, lean):
    if count == 2:
        one = jax.random.randint(stream_key, (), max(1, total - bound), min(bound, total - 1) + 1)
        return jnp.stack([one, total - one])
    tallies = jnp.asarray(length_profile(count, total, bound, lean), jnp.int32)
    couples = (count - 1) // 2
    donor, sink = tallies[1:1 + 2 * couples:2], tallies[2:2 + 2 * couples:2]
    slack = jnp.minimum(donor - 1, bound - sink)
    passed = jax.random.randint(jax.random.fold_in(stream_key, 1), (couples,), 0, 1 << 20) % (slack + 1)
    tallies = tallies.at[1:1 + 2 * couples:2].set(donor - passed).at[2:2 + 2 * couples:2].set(sink + passed)
    return tallies[jax.random.permutation(jax.random.fold_in(stream_key, 2), count)]


def noise(rng, dims, scale, most, cuts=(), kind=jnp.bfloat16):
    result = scale * jax.random.normal(rng, dims, jnp.float32)
    if cuts:
        result = result * levels(rng, dims, cuts, -0.22, 0.18)
    return jnp.clip(result, -most, most).astype(kind)


def noise_with(stream_key, extent, deviation, reach, split, heavy, kind=jnp.bfloat16):
    array = deviation * jax.random.normal(stream_key, extent, jnp.float32)
    if split:
        array = array * levels(stream_key, extent, split, -0.22, 0.18)
    return jnp.clip(spiked(array, jax.random.fold_in(stream_key, 3), *heavy), -reach, reach).astype(kind)


def setup_inputs(seed: int = 0) -> dict:
    seeds = jax.random.split(jax.random.key(seed), 31)
    enc_input = noise(seeds[0], (TOKENS, D), 1.0, 6.0, ((0, 16), (1, 2)))
    dec_input = noise(seeds[1], (TOKENS, D), 1.0, 6.0, ((0, 16), (1, 2)))
    doc_ids = jax.vmap(lambda own: jnp.searchsorted(jnp.cumsum(ragged_sizes(own, DOCS, SEQ, SEQ // 2, 0)), jnp.arange(SEQ), side="right"))(jax.random.split(seeds[2], SEQS)).reshape((SEQS, SEQ)).astype(jnp.int32)
    block_ids = jax.vmap(lambda own: jnp.searchsorted(jnp.cumsum(ragged_sizes(own, NBLOCKS, SEQ, BLOCK, 0)), jnp.arange(SEQ), side="right"))(jax.random.split(seeds[3], SEQS)).reshape((SEQS, SEQ)).astype(jnp.int32)
    enc_qkv_weight = noise(seeds[4], (3, D, D), D ** -0.5, 0.21875, ((1, 2), (2, 16)))
    enc_qv_bias = noise(seeds[5], (2, D), 0.3, 1.5, ((1, 2),))
    enc_out_weight = noise(seeds[6], (D, D), (max(D // 64, 4)) ** -0.5, 1.75, ((0, 2), (1, 16)))
    enc_out_bias = noise(seeds[7], (D,), 0.3, 1.5, ((0, 2),))
    enc_up_weight = noise(seeds[8], (D, FF), D ** -0.5, 0.21875, ((0, 2), (1, 16)))
    enc_up_bias = noise(seeds[9], (FF,), 0.3, 1.5, ((0, 16),))
    enc_down_weight = noise(seeds[10], (FF, D), FF ** -0.5, 0.109375, ((0, 16), (1, 2)))
    enc_down_bias = noise(seeds[11], (D,), 0.3, 1.5, ((0, 2),))
    enc_norm_gain = jnp.clip(1.0 + 0.1 * jax.random.normal(seeds[12], (2, D), jnp.float32), 0.5, 1.5).astype(jnp.bfloat16)
    enc_norm_bias = noise(seeds[13], (2, D), 0.3, 1.5, ((1, 2),))
    self_qkv_weight = noise(seeds[14], (3, D, D), D ** -0.5, 0.21875, ((1, 2), (2, 16)))
    self_qv_bias = noise(seeds[15], (2, D), 0.3, 1.5, ((1, 2),))
    self_out_weight = noise(seeds[16], (D, D), (max(D // 64, 4)) ** -0.5, 1.75, ((0, 2), (1, 16)))
    self_out_bias = noise(seeds[17], (D,), 0.3, 1.5, ((0, 2),))
    cross_qkv_weight = noise(seeds[18], (3, D, D), D ** -0.5, 0.21875, ((1, 2), (2, 16)))
    cross_qv_bias = noise(seeds[19], (2, D), 0.3, 1.5, ((1, 2),))
    cross_out_weight = noise(seeds[20], (D, D), (max(D // 64, 4)) ** -0.5, 1.75, ((0, 2), (1, 16)))
    cross_out_bias = noise(seeds[21], (D,), 0.3, 1.5, ((0, 2),))
    dec_up_weight = noise(seeds[22], (D, FF), D ** -0.5, 0.21875, ((0, 2), (1, 16)))
    dec_up_bias = noise(seeds[23], (FF,), 0.3, 1.5, ((0, 16),))
    dec_down_weight = noise(seeds[24], (FF, D), FF ** -0.5, 0.109375, ((0, 16), (1, 2)))
    dec_down_bias = noise(seeds[25], (D,), 0.3, 1.5, ((0, 2),))
    dec_norm_gain = jnp.clip(1.0 + 0.1 * jax.random.normal(seeds[26], (3, D), jnp.float32), 0.5, 1.5).astype(jnp.bfloat16)
    dec_norm_bias = noise(seeds[27], (3, D), 0.3, 1.5, ((1, 2),))
    enc_cotangent = noise_with(seeds[28], (TOKENS, D), 1.0, 6.0, ((0, 16), (1, 2)), (0, 1, 16, 2.0))
    dec_cotangent = noise_with(seeds[29], (TOKENS, D), 1.0, 6.0, ((0, 16), (1, 2)), (0, 1, 16, 2.0))
    return dict(enc_input=enc_input, dec_input=dec_input, doc_ids=doc_ids, block_ids=block_ids, enc_qkv_weight=enc_qkv_weight, enc_qv_bias=enc_qv_bias, enc_out_weight=enc_out_weight, enc_out_bias=enc_out_bias, enc_up_weight=enc_up_weight, enc_up_bias=enc_up_bias, enc_down_weight=enc_down_weight, enc_down_bias=enc_down_bias, enc_norm_gain=enc_norm_gain, enc_norm_bias=enc_norm_bias, self_qkv_weight=self_qkv_weight, self_qv_bias=self_qv_bias, self_out_weight=self_out_weight, self_out_bias=self_out_bias, cross_qkv_weight=cross_qkv_weight, cross_qv_bias=cross_qv_bias, cross_out_weight=cross_out_weight, cross_out_bias=cross_out_bias, dec_up_weight=dec_up_weight, dec_up_bias=dec_up_bias, dec_down_weight=dec_down_weight, dec_down_bias=dec_down_bias, dec_norm_gain=dec_norm_gain, dec_norm_bias=dec_norm_bias, enc_cotangent=enc_cotangent, dec_cotangent=dec_cotangent)


@jax.custom_vjp
def low(v):
    return lax.optimization_barrier(v.astype(jnp.bfloat16)).astype(jnp.float32)

@jax.custom_vjp
def low_back(v):
    return v

def low_keep(v):
    return (low(v), None)

def low_pass(kept, grad):
    return (grad,)

def back_keep(v):
    return (v, None)

def back_low(kept, grad):
    return (low(grad),)
low.defvjp(low_keep, low_pass)
low_back.defvjp(back_keep, back_low)
HIGH = lax.Precision.HIGHEST
MASKED = -1e+30
EPSILON = 1e-05

def round_pair(value):
    return low(low_back(value))

def product(left, right):
    return jnp.dot(left, right, precision=HIGH)

def layer_norm(resid, gain, shift):
    average = lax.optimization_barrier(jnp.mean(resid, axis=-1, keepdims=True))
    centred = resid - average
    variance = lax.optimization_barrier(jnp.mean(centred * centred, axis=-1, keepdims=True))
    return centred * lax.rsqrt(variance + EPSILON) * gain + shift

def attention(query_low, memory_low, qkv_weight, qv_bias, out_weight, out_bias, doc_ids, block_ids, causal):
    queries = round_pair(product(query_low, qkv_weight[0]) + qv_bias[0])
    key_rows = round_pair(product(memory_low, qkv_weight[1]))
    value_rows = round_pair(product(memory_low, qkv_weight[2]) + qv_bias[1])
    head_shape = (SEQS, SEQ, HEADS, HEAD_DIM)

    def one_sequence(sequence_item):
        seq_queries, seq_keys, seq_values, seq_docs, seq_blocks = sequence_item
        allowed = seq_docs[:, None] == seq_docs[None, :]
        if causal:
            allowed = jnp.logical_and(allowed, seq_blocks[None, :] <= seq_blocks[:, None])
        scores = low_back(jnp.einsum('qhd,khd->hqk', seq_queries, seq_keys, precision=HIGH) * HEAD_DIM ** (-0.5))
        scores = jnp.where(allowed[None], scores, MASKED)
        maxima = lax.optimization_barrier(jnp.max(scores, axis=-1, keepdims=True))
        powered = jnp.exp(scores - maxima)
        weights = low(powered / lax.optimization_barrier(jnp.sum(powered, axis=-1, keepdims=True)))
        return jnp.einsum('hqk,khd->qhd', weights, seq_values, precision=HIGH)
    mixture = lax.map(jax.checkpoint(one_sequence), (queries.reshape(head_shape), key_rows.reshape(head_shape), value_rows.reshape(head_shape), doc_ids, block_ids))
    mixture = round_pair(mixture.reshape(SEQS * SEQ, D))
    return low_back(product(mixture, out_weight) + out_bias)

def feed_forward(source_low, up_weight, up_bias, down_weight, down_bias):
    preact = low_back(product(source_low, up_weight) + up_bias)
    hidden = low(jax.nn.gelu(preact, approximate=False))
    return low_back(product(hidden, down_weight) + down_bias)

def encoder(source, params, doc_ids, block_ids):
    qkv_weight, qv_bias, out_weight, out_bias, up_weight, up_bias, down_weight, down_bias, gain_rows, shift_rows = params
    branch_one = attention(source, source, qkv_weight, qv_bias, out_weight, out_bias, doc_ids, block_ids, False)
    first_out = layer_norm(source + branch_one, gain_rows[0], shift_rows[0])
    branch_two = feed_forward(low(first_out), up_weight, up_bias, down_weight, down_bias)
    return layer_norm(first_out + branch_two, gain_rows[1], shift_rows[1])

def decoder(target, memory, params, doc_ids, block_ids):
    self_qkv, self_qv, self_out, self_bias, cross_qkv, cross_qv, cross_out, cross_bias, up_weight, up_bias, down_weight, down_bias, gain_rows, shift_rows = params
    memory_low = low(memory)
    branch_one = attention(target, target, self_qkv, self_qv, self_out, self_bias, doc_ids, block_ids, True)
    first_out = layer_norm(target + branch_one, gain_rows[0], shift_rows[0])
    branch_two = attention(low(first_out), memory_low, cross_qkv, cross_qv, cross_out, cross_bias, doc_ids, block_ids, False)
    second_out = layer_norm(first_out + branch_two, gain_rows[1], shift_rows[1])
    branch_three = feed_forward(low(second_out), up_weight, up_bias, down_weight, down_bias)
    return layer_norm(second_out + branch_three, gain_rows[2], shift_rows[2])

def reference(enc_input, dec_input, doc_ids, block_ids, enc_qkv_weight, enc_qv_bias, enc_out_weight, enc_out_bias, enc_up_weight, enc_up_bias, enc_down_weight, enc_down_bias, enc_norm_gain, enc_norm_bias, self_qkv_weight, self_qv_bias, self_out_weight, self_out_bias, cross_qkv_weight, cross_qv_bias, cross_out_weight, cross_out_bias, dec_up_weight, dec_up_bias, dec_down_weight, dec_down_bias, dec_norm_gain, dec_norm_bias, enc_cotangent, dec_cotangent):
    enc_params = tuple((weight_arg.astype(jnp.float32) for weight_arg in (enc_qkv_weight, enc_qv_bias, enc_out_weight, enc_out_bias, enc_up_weight, enc_up_bias, enc_down_weight, enc_down_bias, enc_norm_gain, enc_norm_bias)))
    dec_params = tuple((weight_arg.astype(jnp.float32) for weight_arg in (self_qkv_weight, self_qv_bias, self_out_weight, self_out_bias, cross_qkv_weight, cross_qv_bias, cross_out_weight, cross_out_bias, dec_up_weight, dec_up_bias, dec_down_weight, dec_down_bias, dec_norm_gain, dec_norm_bias)))

    def forward(enc_source, dec_source, enc_set, dec_set):
        memory = encoder(enc_source, enc_set, doc_ids, block_ids)
        return (memory, decoder(dec_source, memory, dec_set, doc_ids, block_ids))
    outputs, pullback = jax.vjp(forward, enc_input.astype(jnp.float32), dec_input.astype(jnp.float32), enc_params, dec_params)
    grad_enc, grad_dec, enc_grads, dec_grads = pullback((enc_cotangent.astype(jnp.float32), dec_cotangent.astype(jnp.float32)))
    return (outputs[0].astype(jnp.bfloat16), outputs[1].astype(jnp.bfloat16), grad_enc, grad_dec, enc_grads[0], enc_grads[1], enc_grads[2], enc_grads[3], enc_grads[4], enc_grads[5], enc_grads[6], enc_grads[7], enc_grads[8], enc_grads[9], dec_grads[0], dec_grads[1], dec_grads[2], dec_grads[3], dec_grads[4], dec_grads[5], dec_grads[6], dec_grads[7], dec_grads[8], dec_grads[9], dec_grads[10], dec_grads[11], dec_grads[12], dec_grads[13])
```

```python
import jax
import jax.numpy as jnp
from jax import lax
from jax.sharding import PartitionSpec as P

HEAD_DIM = 64
EPSILON = 1e-05
MASKED = -1e30
bf16 = jnp.bfloat16
f32 = jnp.float32


def nt(left, right):
    return lax.dot_general(left, right, (((1,), (1,)), ((), ())), preferred_element_type=f32)


def nn(left, right):
    return lax.dot_general(left, right, (((1,), (0,)), ((), ())), preferred_element_type=f32)


def tn(left, right):
    return lax.dot_general(left, right, (((0,), (0,)), ((), ())), preferred_element_type=f32)


def gy_swap(block, mask):
    count = lax.axis_size("gy")
    return lax.ppermute(block, "gy", [(i, i ^ mask) for i in range(count)])


def gx_swap(block):
    return lax.ppermute(block, "gx", [(0, 1), (1, 0)])


def gx_sum(partial):
    return partial + gx_swap(partial.astype(bf16)).astype(f32)


def gx_first():
    return lax.axis_index("gx") == 0


def gx_join(own, axis):
    other = gx_swap(own)
    first = gx_first()
    return jnp.concatenate(
        [jnp.where(first, own, other), jnp.where(first, other, own)], axis=axis
    )


def gx_half(full):
    middle = full.shape[-1] // 2
    return jnp.where(gx_first(), full[..., :middle], full[..., middle:])


def gx_trade(pair):
    first = gx_first()
    own = jnp.where(first, pair[0], pair[1])
    other = gx_swap(jnp.where(first, pair[1], pair[0]))
    return jnp.where(first, own, other), jnp.where(first, other, own)


def diagonal_swap(block):
    count = lax.axis_size("gy")
    middle = count // 2
    route = []
    for low in range(middle):
        route += [(middle + low, count + low), (count + low, middle + low)]
    other = lax.ppermute(block, ("gx", "gy"), route)
    upper = lax.axis_index("gy") >= middle
    moved = jnp.logical_xor(upper, lax.axis_index("gx") == 1)
    return jnp.where(moved, other, block)


def masks_down(count):
    return [1 << bit for bit in reversed(range(count.bit_length() - 1))]


def masks_up(count):
    return [1 << bit for bit in range(count.bit_length() - 1)]


def gather_ordered(block, count):
    device = lax.axis_index("gy")
    stack = block[None]
    for mask in masks_down(count):
        other = gy_swap(stack, mask)
        lower = device // mask % 2 == 0
        stack = jnp.stack(
            [jnp.where(lower, stack, other), jnp.where(lower, other, stack)], axis=1
        ).reshape((-1,) + block.shape)
    return stack


def reduce_ordered(stack, count):
    device = lax.axis_index("gy")
    for mask in masks_up(count):
        pair = stack.reshape((stack.shape[0] // 2, 2) + stack.shape[1:])
        lower = device // mask % 2 == 0
        kept = jnp.where(lower, pair[:, 0], pair[:, 1])
        sent = jnp.where(lower, pair[:, 1], pair[:, 0])
        stack = kept.astype(f32) + gy_swap(sent.astype(bf16), mask).astype(f32)
    return stack[0]


def gather_xor(block):
    stack = block
    for mask in masks_down(lax.axis_size("gy")):
        stack = jnp.concatenate([stack, gy_swap(stack, mask)], axis=0)
    return stack


def reduce_xor(stack, wire=bf16):
    for mask in masks_up(lax.axis_size("gy")):
        middle = stack.shape[0] // 2
        stack = stack[:middle].astype(f32) + gy_swap(stack[middle:].astype(wire), mask).astype(
            f32
        )
    return stack


def all_sum(vector):
    for mask in masks_up(lax.axis_size("gy")):
        vector = vector + gy_swap(vector, mask)
    return vector


def fetch_attention(qkv_weight, out_weight):
    moved = diagonal_swap(jnp.swapaxes(qkv_weight, 1, 2))
    block = jnp.concatenate([moved, out_weight.T[None]], axis=0)
    count = lax.axis_size("gy")
    stack = gather_ordered(block, count)
    columns, rows = block.shape[1:]
    wide = stack[:, :3].reshape(2, count // 2, 3, columns, rows)
    wide = wide.transpose(2, 1, 3, 0, 4).reshape(3, count // 2 * columns, 2 * rows)
    return wide, stack[:, 3].reshape(count * columns, rows)


def return_attention(grad_wide, grad_out):
    count = lax.axis_size("gy")
    _, half, width = grad_wide.shape
    columns = width // count
    stack = grad_wide.reshape(3, count // 2, columns, 2, half).transpose(3, 1, 0, 2, 4)
    stack = stack.reshape(count, 3, columns, half)
    stack = jnp.concatenate([stack, grad_out.reshape(count, 1, columns, half)], axis=1)
    block = reduce_ordered(stack, count)
    moved = diagonal_swap(block[:3].astype(bf16)).astype(f32)
    return jnp.swapaxes(moved, 1, 2), block[3].T


def fetch_feed(up_weight, up_bias, down_weight):
    half = up_bias.shape[0] // 2
    up_low, up_high = gx_trade(up_weight.T.reshape(2, half, -1))
    down_low, down_high = gx_trade(down_weight.reshape(2, half, -1))
    bias = jnp.where(gx_first(), up_bias[:half], up_bias[half:])
    up_full = gather_xor(jnp.concatenate([up_low, up_high], axis=1))
    down_full = gather_xor(jnp.concatenate([down_low, down_high], axis=1))
    return up_full, gather_xor(bias), down_full


def return_feed(grad_up, grad_down):
    up_block = reduce_xor(grad_up).astype(bf16)
    down_block = reduce_xor(grad_down).astype(bf16)
    middle = up_block.shape[1] // 2
    up_pair = gx_trade((up_block[:, :middle], up_block[:, middle:]))
    down_pair = gx_trade((down_block[:, :middle], down_block[:, middle:]))
    up_grad = jnp.concatenate(up_pair, axis=0).astype(f32).T
    return up_grad, jnp.concatenate(down_pair, axis=0).astype(f32)


def norm_forward(resid, gain, shift):
    average = jnp.mean(resid, axis=1, keepdims=True)
    centred = resid - average
    factor = lax.rsqrt(jnp.mean(centred * centred, axis=1, keepdims=True) + EPSILON)
    normed = centred * factor
    return normed * gain.astype(f32) + shift.astype(f32), (normed, factor)


def norm_backward(grad_out, saved, gain):
    normed, factor = saved
    scaled = grad_out * gain.astype(f32)
    middle = jnp.mean(scaled, axis=1, keepdims=True)
    along = jnp.mean(scaled * normed, axis=1, keepdims=True)
    grad_in = factor * (scaled - middle - normed * along)
    return grad_in, gx_half(jnp.sum(grad_out * normed, axis=0)), gx_half(jnp.sum(grad_out, axis=0))


def heads_of(array):
    return array.reshape(array.shape[0], -1, HEAD_DIM)


def attend_forward(queries, keys, values, allowed):
    rows, features = queries.shape
    scores = jnp.einsum(
        "qhd,khd->hqk", heads_of(queries), heads_of(keys), preferred_element_type=f32
    ) * HEAD_DIM ** (-0.5)
    scores = jnp.where(allowed[None], scores, MASKED)
    maxima = jnp.max(scores, axis=2, keepdims=True)
    powered = jnp.exp(scores - maxima)
    totals = jnp.sum(powered, axis=2, keepdims=True)
    weights = (powered / totals).astype(bf16)
    mixture = jnp.einsum("hqk,khd->qhd", weights, heads_of(values), preferred_element_type=f32)
    return mixture.reshape(rows, features).astype(bf16), maxima + jnp.log(totals)


def attend_backward(queries, keys, values, allowed, logsum, grad_mixture):
    rows, features = queries.shape
    factor = HEAD_DIM ** (-0.5)
    portion, grad_part = heads_of(queries), heads_of(grad_mixture)
    keys_all, values_all = heads_of(keys), heads_of(values)
    scores = (
        jnp.einsum("qhd,khd->hqk", portion, keys_all, preferred_element_type=f32) * factor
    )
    scores = jnp.where(allowed[None], scores, MASKED)
    probs = jnp.exp(scores - logsum)
    weights = probs.astype(bf16)
    grad_probs = jnp.einsum("qhd,khd->hqk", grad_part, values_all, preferred_element_type=f32)
    deltas = jnp.sum(probs * grad_probs, axis=2, keepdims=True)
    grad_scores = (probs * (grad_probs - deltas)).astype(bf16)
    grad_queries = (
        jnp.einsum("hqk,khd->qhd", grad_scores, keys_all, preferred_element_type=f32) * factor
    )
    grad_keys = (
        jnp.einsum("hqk,qhd->khd", grad_scores, portion, preferred_element_type=f32) * factor
    )
    grad_values = jnp.einsum("hqk,qhd->khd", weights, grad_part, preferred_element_type=f32)
    grad_pairs = jnp.concatenate(
        [grad_keys.reshape(-1, features), grad_values.reshape(-1, features)], axis=1
    )
    return grad_queries.reshape(rows, features).astype(bf16), grad_pairs.astype(bf16)


def attention_forward(source, memory, weights, qv_bias, out_bias, allowed, group):
    wide, out_full = weights
    half = wide.shape[1]
    flat = wide.reshape(3 * half, -1)
    biases = qv_bias.astype(f32)
    if source is memory:
        summed = nt(source, flat)
        query_sum, key_sum, value_sum = (
            summed[:, :half], summed[:, half:2 * half], summed[:, 2 * half:]
        )
    else:
        query_sum = nt(source, flat[:half])
        pairs_sum = nt(memory, flat[half:])
        key_sum, value_sum = pairs_sum[:, :half], pairs_sum[:, half:]
    queries = (query_sum + biases[0]).astype(bf16)
    pairs = jnp.concatenate([key_sum.astype(bf16), (value_sum + biases[1]).astype(bf16)], axis=1)
    pairs = gather_ordered(pairs, group).reshape(-1, 2 * half)
    keys, values = pairs[:, :half], pairs[:, half:]
    mixture, logsum = attend_forward(queries, keys, values, allowed)
    branch = gx_sum(nt(mixture, out_full)) + out_bias.astype(f32)
    return branch, (source, memory, queries, keys, values, mixture, logsum)


def attention_backward(grad_branch, weights, allowed, group, saved):
    wide, out_full = weights
    half = wide.shape[1]
    flat = wide.reshape(3 * half, -1)
    source, memory, queries, keys, values, mixture, logsum = saved
    grad_round = grad_branch.astype(bf16)
    grad_out_bias = gx_half(jnp.sum(grad_round.astype(f32), axis=0))
    grad_mixture = nn(grad_round, out_full).astype(bf16)
    grad_out = tn(grad_round, mixture).astype(bf16)
    grad_queries, grad_pairs = attend_backward(
        queries, keys, values, allowed, logsum, grad_mixture
    )
    grad_pairs = reduce_ordered(
        grad_pairs.reshape(group, -1, 2 * half), group
    ).astype(bf16)
    grad_qv = jnp.stack(
        [
            jnp.sum(grad_queries.astype(f32), axis=0),
            jnp.sum(grad_pairs[:, half:].astype(f32), axis=0),
        ]
    )
    if source is memory:
        joined = jnp.concatenate([grad_queries, grad_pairs], axis=1)
        grad_source = gx_sum(nn(joined, flat))
        grad_memory = None
        grad_wide = tn(joined, source).astype(bf16)
    else:
        grad_source = gx_sum(nn(grad_queries, flat[:half]))
        grad_memory = gx_sum(nn(grad_pairs, flat[half:]))
        grad_wide = jnp.concatenate(
            [tn(grad_queries, source).astype(bf16), tn(grad_pairs, memory).astype(bf16)], axis=0
        )
    large = return_attention(grad_wide.reshape(3, half, -1), grad_out)
    return grad_source, grad_memory, large, grad_qv, grad_out_bias


def feed_forward(source, weights, down_bias):
    up_full, up_bias, down_full = weights
    preact = nt(source, up_full) + up_bias.astype(f32)
    hidden = jax.nn.gelu(preact, approximate=False).astype(bf16)
    branch = gx_sum(nn(hidden, down_full)) + down_bias.astype(f32)
    return branch, (source, preact, hidden)


def feed_backward(grad_branch, weights, saved):
    up_full, up_bias, down_full = weights
    source, preact, hidden = saved
    grad_round = grad_branch.astype(bf16)
    grad_down_bias = gx_half(jnp.sum(grad_round.astype(f32), axis=0))
    grad_hidden = nt(grad_round, down_full)
    pullback = jax.vjp(lambda v: jax.nn.gelu(v, approximate=False), preact)[1]
    grad_preact = pullback(grad_hidden)[0].astype(bf16)
    grad_source = gx_sum(nn(grad_preact, up_full))
    grad_down = tn(hidden, grad_round).astype(bf16)
    grad_up = tn(grad_preact, source).astype(bf16)
    grad_up_bias = jnp.sum(grad_preact.astype(f32), axis=0)
    large = return_feed(grad_up, grad_down)
    return grad_source, large, grad_up_bias, grad_down_bias


def per_device(
    enc_input,
    dec_input,
    doc_ids,
    block_ids,
    enc_qkv_weight,
    enc_qv_bias,
    enc_out_weight,
    enc_out_bias,
    enc_up_weight,
    enc_up_bias,
    enc_down_weight,
    enc_down_bias,
    enc_norm_gain,
    enc_norm_bias,
    self_qkv_weight,
    self_qv_bias,
    self_out_weight,
    self_out_bias,
    cross_qkv_weight,
    cross_qv_bias,
    cross_out_weight,
    cross_out_bias,
    dec_up_weight,
    dec_up_bias,
    dec_down_weight,
    dec_down_bias,
    dec_norm_gain,
    dec_norm_bias,
    enc_cotangent,
    dec_cotangent,
):
    rows = enc_input.shape[0]
    sequence = doc_ids.shape[1]
    group = sequence // rows
    device = lax.axis_index("gy")
    offset = device % group * rows
    docs_row = lax.dynamic_index_in_dim(doc_ids, device // group, 0, keepdims=False)
    blocks_row = lax.dynamic_index_in_dim(block_ids, device // group, 0, keepdims=False)
    query_docs = lax.dynamic_slice_in_dim(docs_row, offset, rows)
    query_blocks = lax.dynamic_slice_in_dim(blocks_row, offset, rows)
    same_doc = query_docs[:, None] == docs_row[None, :]
    causal = jnp.logical_and(same_doc, blocks_row[None, :] <= query_blocks[:, None])

    enc_low = gx_join(enc_input, 1)
    enc_attn = fetch_attention(enc_qkv_weight, enc_out_weight)
    vectors = gx_join(
        jnp.concatenate(
            [
                enc_out_bias[None],
                enc_down_bias[None],
                self_out_bias[None],
                cross_out_bias[None],
                dec_down_bias[None],
                enc_norm_gain,
                enc_norm_bias,
                dec_norm_gain,
                dec_norm_bias,
            ],
            axis=0,
        ),
        1,
    )
    enc_gain, enc_shift = vectors[5:7], vectors[7:9]
    dec_gain, dec_shift = vectors[9:12], vectors[12:15]
    dec_low = gx_join(dec_input, 1)
    enc_feed = fetch_feed(enc_up_weight, enc_up_bias, enc_down_weight)
    self_attn = fetch_attention(self_qkv_weight, self_out_weight)
    cross_attn = fetch_attention(cross_qkv_weight, cross_out_weight)
    dec_feed = fetch_feed(dec_up_weight, dec_up_bias, dec_down_weight)
    cotangents = gx_join(jnp.stack([enc_cotangent, dec_cotangent]), 2).astype(f32)

    branch, enc_attn_saved = attention_forward(
        enc_low, enc_low, enc_attn, enc_qv_bias, vectors[0], same_doc, group
    )
    x1, x1_norm = norm_forward(enc_low.astype(f32) + branch, enc_gain[0], enc_shift[0])
    branch, enc_feed_saved = feed_forward(x1.astype(bf16), enc_feed, vectors[1])
    x2, x2_norm = norm_forward(x1 + branch, enc_gain[1], enc_shift[1])
    memory = x2.astype(bf16)

    branch, self_saved = attention_forward(
        dec_low, dec_low, self_attn, self_qv_bias, vectors[2], causal, group
    )
    y1, y1_norm = norm_forward(dec_low.astype(f32) + branch, dec_gain[0], dec_shift[0])
    branch, cross_saved = attention_forward(
        y1.astype(bf16), memory, cross_attn, cross_qv_bias, vectors[3], same_doc, group
    )
    y2, y2_norm = norm_forward(y1 + branch, dec_gain[1], dec_shift[1])
    branch, dec_feed_saved = feed_forward(y2.astype(bf16), dec_feed, vectors[4])
    y3, y3_norm = norm_forward(y2 + branch, dec_gain[2], dec_shift[2])

    g3, gain_d2, shift_d2 = norm_backward(cotangents[1], y3_norm, dec_gain[2])
    grad, dec_feed_large, dec_up_grad, dec_down_grad = feed_backward(g3, dec_feed, dec_feed_saved)
    g2, gain_d1, shift_d1 = norm_backward(g3 + grad, y2_norm, dec_gain[1])
    grad, grad_memory, cross_large, cross_qv_grad, cross_out_grad = attention_backward(
        g2, cross_attn, same_doc, group, cross_saved
    )
    g1, gain_d0, shift_d0 = norm_backward(g2 + grad, y1_norm, dec_gain[0])
    grad, _, self_large, self_qv_grad, self_out_grad = attention_backward(
        g1, self_attn, causal, group, self_saved
    )
    dec_input_grad = gx_half(g1 + grad)

    e2, gain_e1, shift_e1 = norm_backward(cotangents[0] + grad_memory, x2_norm, enc_gain[1])
    grad, enc_feed_large, enc_up_grad, enc_down_grad = feed_backward(e2, enc_feed, enc_feed_saved)
    e1, gain_e0, shift_e0 = norm_backward(e2 + grad, x1_norm, enc_gain[0])
    grad, _, enc_large, enc_qv_grad, enc_out_grad = attention_backward(
        e1, enc_attn, same_doc, group, enc_attn_saved
    )
    enc_input_grad = gx_half(e1 + grad)

    up_sums = reduce_xor(
        jnp.stack(
            [
                enc_up_grad.reshape(lax.axis_size("gy"), -1),
                dec_up_grad.reshape(lax.axis_size("gy"), -1),
            ],
            axis=1,
        ),
        f32,
    )[0]
    up_sums = gx_join(up_sums, 1)
    sums = all_sum(
        jnp.concatenate(
            [
                jnp.stack([gain_e0, gain_e1, shift_e0, shift_e1]),
                jnp.stack([gain_d0, gain_d1, gain_d2, shift_d0, shift_d1, shift_d2]),
                jnp.stack([enc_out_grad, enc_down_grad]),
                jnp.stack([self_out_grad, cross_out_grad, dec_down_grad]),
                enc_qv_grad,
                self_qv_grad,
                cross_qv_grad,
            ],
            axis=0,
        )
    )
    return (
        gx_half(memory),
        gx_half(y3.astype(bf16)),
        enc_input_grad,
        dec_input_grad,
        enc_large[0],
        sums[15:17],
        enc_large[1],
        sums[10],
        enc_feed_large[0],
        up_sums[0],
        enc_feed_large[1],
        sums[11],
        sums[0:2],
        sums[2:4],
        self_large[0],
        sums[17:19],
        self_large[1],
        sums[12],
        cross_large[0],
        sums[19:21],
        cross_large[1],
        sums[13],
        dec_feed_large[0],
        up_sums[1],
        dec_feed_large[1],
        sums[14],
        sums[4:7],
        sums[7:10],
    )


def solution(mesh):
    return jax.shard_map(
        per_device,
        mesh=mesh,
        in_specs=(
            P("gy", "gx"),
            P("gy", "gx"),
            P(),
            P(),
            P(None, "gx", "gy"),
            P(None, "gx"),
            P("gx", "gy"),
            P("gx"),
            P("gx", "gy"),
            P("gy"),
            P("gy", "gx"),
            P("gx"),
            P(None, "gx"),
            P(None, "gx"),
            P(None, "gx", "gy"),
            P(None, "gx"),
            P("gx", "gy"),
            P("gx"),
            P(None, "gx", "gy"),
            P(None, "gx"),
            P("gx", "gy"),
            P("gx"),
            P("gx", "gy"),
            P("gy"),
            P("gy", "gx"),
            P("gx"),
            P(None, "gx"),
            P(None, "gx"),
            P("gy", "gx"),
            P("gy", "gx"),
        ),
        out_specs=(
            P("gy", "gx"),
            P("gy", "gx"),
            P("gy", "gx"),
            P("gy", "gx"),
            P(None, "gx", "gy"),
            P(None, "gx"),
            P("gx", "gy"),
            P("gx"),
            P("gx", "gy"),
            P("gy"),
            P("gy", "gx"),
            P("gx"),
            P(None, "gx"),
            P(None, "gx"),
            P(None, "gx", "gy"),
            P(None, "gx"),
            P("gx", "gy"),
            P("gx"),
            P(None, "gx", "gy"),
            P(None, "gx"),
            P("gx", "gy"),
            P("gx"),
            P("gx", "gy"),
            P("gy"),
            P("gy", "gx"),
            P("gx"),
            P(None, "gx"),
            P(None, "gx"),
        ),
        check_vma=False,
    )
```

```python
import jax
import jax.numpy as jnp
from jax import lax
from jax.experimental import pallas as pl
from jax.experimental.pallas import tpu as pltpu
from jax.sharding import PartitionSpec as P

HEAD_DIM = 64
EPSILON = 1e-05
MASKED = -1e30
bf16 = jnp.bfloat16
f32 = jnp.float32


def nt(left, right):
    return lax.dot_general(left, right, (((1,), (1,)), ((), ())), preferred_element_type=f32)


def nn(left, right):
    return lax.dot_general(left, right, (((1,), (0,)), ((), ())), preferred_element_type=f32)


def tn(left, right):
    return lax.dot_general(left, right, (((0,), (0,)), ((), ())), preferred_element_type=f32)


def gy_swap(block, mask):
    count = lax.axis_size("gy")
    return lax.ppermute(block, "gy", [(i, i ^ mask) for i in range(count)])


def gx_swap(block):
    return lax.ppermute(block, "gx", [(0, 1), (1, 0)])


def gx_sum(partial):
    return partial + gx_swap(partial.astype(bf16)).astype(f32)


def gx_first():
    return lax.axis_index("gx") == 0


def gx_join(own, axis):
    other = gx_swap(own)
    first = gx_first()
    return jnp.concatenate(
        [jnp.where(first, own, other), jnp.where(first, other, own)], axis=axis
    )


def gx_half(full):
    middle = full.shape[-1] // 2
    return jnp.where(gx_first(), full[..., :middle], full[..., middle:])


def diagonal_send(block):
    count = lax.axis_size("gy")
    middle = count // 2
    route = []
    for low in range(middle):
        route += [(middle + low, count + low), (count + low, middle + low)]
    return lax.ppermute(block, ("gx", "gy"), route)


def diagonal_keep(own, other):
    upper = lax.axis_index("gy") >= lax.axis_size("gy") // 2
    return jnp.where(jnp.logical_xor(upper, lax.axis_index("gx") == 1), other, own)


def masks_down(count):
    return [1 << bit for bit in reversed(range(count.bit_length() - 1))]


def masks_up(count):
    return [1 << bit for bit in range(count.bit_length() - 1)]


def gather_group(block, count):
    masks = masks_down(count)
    for mask in masks[:-1]:
        block = jnp.concatenate([block, gy_swap(block, mask)], axis=0)
    return block, gy_swap(block, masks[-1])


def reduce_group(kept, sent, count):
    for mask in masks_up(count):
        if mask > 1:
            middle = kept.shape[0] // 2
            kept, sent = kept[:middle], kept[middle:].astype(bf16)
        kept = kept.astype(f32) + gy_swap(sent, mask).astype(f32)
    return kept[0].astype(bf16)


def group_order(values, count, rows):
    device = lax.axis_index("gy") % count
    positions = [0]
    for mask in masks_down(count):
        positions = positions + [position ^ mask for position in positions]
    parts = [
        lax.dynamic_slice_in_dim(values, (device ^ position) * rows, rows)
        for position in positions
    ]
    return jnp.concatenate(parts)


class Task:
    def __init__(self, chain):
        self.chain = chain
        self.result = None
        self.pending = next(chain)

    def advance(self, arrived):
        try:
            self.pending = self.chain.send(arrived)
        except StopIteration as stop:
            self.pending = None
            self.result = stop.value

    def finish(self):
        while self.pending is not None:
            self.advance(self.pending)
        return self.result


def tick(act, *tasks):
    live = [task for task in tasks if task.pending is not None]
    if not live:
        return act
    tied = lax.optimization_barrier((act,) + tuple(task.pending for task in live))
    for task, arrived in zip(live, tied[1:]):
        task.advance(arrived)
    return tied[0]


def launch(act, *tasks):
    for task in tasks:
        if task.pending is not None:
            task.advance(lax.optimization_barrier((act, task.pending))[1])
    return act


def link_order(count, x_first=False):
    masks = masks_down(count)
    if not x_first:
        return masks
    return [mask for mask in masks if mask == 2] + [mask for mask in masks if mask != 2]


def gather_chain(stack):
    device = lax.axis_index("gy")
    matrices, columns, width = stack.shape
    present = []
    for mask in link_order(lax.axis_size("gy")):
        other = yield gy_swap(stack, mask)
        above = len([there for there in present if there > mask])
        shape = (matrices, 1 << above, -1, columns, width)
        own, other = stack.reshape(shape), other.reshape(shape)
        lower = device // mask % 2 == 0
        stack = jnp.stack(
            [jnp.where(lower, own, other), jnp.where(lower, other, own)], axis=2
        ).reshape(matrices, -1, width)
        present.append(mask)
    return stack


def attention_fetch(qkv_weight, out_weight):
    qkv_weight, out_weight = yield (qkv_weight, out_weight)
    own = jnp.swapaxes(qkv_weight, 1, 2)
    moved = diagonal_keep(own, (yield diagonal_send(own)))
    block = jnp.concatenate([moved, out_weight.T[None]], axis=0)
    stack = yield from gather_chain(block)
    half = stack.shape[1] // 2
    wide = jnp.concatenate([stack[:3, :half], stack[:3, half:]], axis=2)
    return wide.reshape(3 * half, 2 * half), stack[3]


def attention_return(grad_wide, grad_out, x_last=False):
    count = lax.axis_size("gy")
    device = lax.axis_index("gy")
    half = grad_out.shape[1]
    columns = grad_out.shape[0] // count
    stack = jnp.concatenate([grad_wide.reshape(3, -1, half), grad_out[None]], axis=0)
    stack = yield stack
    present = masks_down(count)
    for mask in reversed(link_order(count, x_last)):
        above = len([there for there in present if there > mask])
        pair = stack.reshape(4, 1 << above, 2, -1, columns, half)
        lower = device // mask % 2 == 0
        kept = jnp.where(lower, pair[:, :, 0], pair[:, :, 1])
        sent = jnp.where(lower, pair[:, :, 1], pair[:, :, 0])
        other = yield gy_swap(sent.astype(bf16), mask)
        stack = kept.astype(f32) + other.astype(f32)
        present.remove(mask)
    block = stack.reshape(4, columns, half)
    own = block[:3].astype(bf16)
    moved = diagonal_keep(own, (yield diagonal_send(own)))
    return jnp.swapaxes(moved.astype(f32), 1, 2), block[3].T


def trade_send(pair):
    first = gx_first()
    return jnp.where(first, pair[0], pair[1]), gx_swap(jnp.where(first, pair[1], pair[0]))


def trade_keep(own, other, axis):
    first = gx_first()
    return jnp.concatenate(
        [jnp.where(first, own, other), jnp.where(first, other, own)], axis=axis
    )


def feed_fetch(stack):
    stack = yield stack
    for mask in link_order(lax.axis_size("gy")):
        other = yield gy_swap(stack, mask)
        if mask > 1:
            stack = jnp.concatenate([stack, other], axis=1)
    return (stack[0], other[0]), (stack[1], other[1])


def true_order(blocks):
    masks = link_order(blocks.shape[0])
    wanted = lax.axis_index("gy") ^ jnp.arange(blocks.shape[0])
    places = sum(((wanted // mask) % 2) * (1 << level) for level, mask in enumerate(masks))
    return jnp.take(blocks, places, axis=0)


def feed_return(up_pair, down_pair):
    up_pair, down_pair = yield (up_pair, down_pair)
    up_other, down_other = yield (gy_swap(up_pair[1], 1), gy_swap(down_pair[1], 1))
    stack = jnp.stack(
        [
            up_pair[0].astype(f32) + up_other.astype(f32),
            down_pair[0].astype(f32) + down_other.astype(f32),
        ]
    )
    for mask in list(reversed(link_order(lax.axis_size("gy"))))[1:]:
        middle = stack.shape[1] // 2
        other = yield gy_swap(stack[:, middle:].astype(bf16), mask)
        stack = stack[:, :middle].astype(f32) + other.astype(f32)
    return (yield from feed_trade(stack))


def feed_trade(stack):
    stack = stack.astype(bf16)
    middle = stack.shape[2] // 2
    own, other = trade_send((stack[:, :, :middle], stack[:, :, middle:]))
    other = yield other
    both = trade_keep(own, other, 1).astype(f32)
    return both[0].T, both[1]


def join_chain(own, axis):
    own = yield own
    other = yield gx_swap(own)
    return trade_keep(own, other, axis)


def sum_chain(vector, columns):
    vector = yield vector
    for mask in masks_up(lax.axis_size("gy")):
        other = yield gy_swap(vector, mask)
        vector = vector + other
    blocks = vector[21:].reshape(2, -1, columns)
    own = lax.dynamic_index_in_dim(blocks, lax.axis_index("gy"), 1, keepdims=False)
    other = yield gx_swap(own)
    return vector, trade_keep(own, other, 1)


def hidden_forward(source, weights, lane):
    ups, downs = weights
    lanes = lax.broadcasted_iota(jnp.int32, (source.shape[0], LANES), 1)
    widened = jnp.concatenate([source, (lanes == lane).astype(bf16)], axis=1)
    pres = [nt(widened, up) for up in ups]
    hiddens = [jax.nn.gelu(pre, approximate=False).astype(bf16) for pre in pres]
    width = source.shape[1]
    partial = sum(nn(hidden, down[:, :width]) for hidden, down in zip(hiddens, downs))
    return gx_sum(partial), pres, hiddens


def hidden_backward(grad_round, weights, pres):
    ups, downs = weights
    width = grad_round.shape[1]
    grad_pres = []
    for pre, down in zip(pres, downs):
        pullback = jax.vjp(lambda v: jax.nn.gelu(v, approximate=False), pre)[1]
        grad_pres.append(pullback(nt(grad_round, down[:, :width]))[0].astype(bf16))
    partial = sum(nn(grad_pre, up[:, :width]) for grad_pre, up in zip(grad_pres, ups))
    return grad_pres, gx_sum(partial)


def hidden_grads(grad_pres, hiddens, source, grad_round):
    return (
        tuple(tn(grad_pre, source).astype(bf16) for grad_pre in grad_pres),
        tuple(tn(hidden, grad_round).astype(bf16) for hidden in hiddens),
    )


def norm_forward(resid, gain, shift):
    average = jnp.mean(resid, axis=1, keepdims=True)
    centred = resid - average
    factor = lax.rsqrt(jnp.mean(centred * centred, axis=1, keepdims=True) + EPSILON)
    normed = centred * factor
    return normed * gain.astype(f32) + shift.astype(f32), (normed, factor)


def norm_backward(grad_out, saved, gain):
    normed, factor = saved
    scaled = grad_out * gain.astype(f32)
    middle = jnp.mean(scaled, axis=1, keepdims=True)
    along = jnp.mean(scaled * normed, axis=1, keepdims=True)
    grad_in = factor * (scaled - middle - normed * along)
    return grad_in, gx_half(jnp.sum(grad_out * normed, axis=0)), gx_half(jnp.sum(grad_out, axis=0))


LANES = 128


def allowed_of(query_ids, key_ids, causal):
    allowed = query_ids[0][...] == key_ids[0:1, :]
    if causal:
        allowed = jnp.logical_and(allowed, key_ids[1:2, :] <= query_ids[1][...])
    return allowed


def lane_masks():
    lanes = lax.broadcasted_iota(jnp.int32, (1, LANES), 1)
    count = LANES // HEAD_DIM
    return [
        jnp.logical_and(lanes >= HEAD_DIM * head, lanes < HEAD_DIM * (head + 1))
        for head in range(count)
    ]


def kernel_forward(
    causal, query, low_key, high_key, low_value, high_value, docs, blocks, ids, mixture, logsum
):
    allowed = allowed_of((docs, blocks), ids[...], causal)
    keys = jnp.concatenate([low_key[...], high_key[...]], axis=0)
    values = jnp.concatenate([low_value[...], high_value[...]], axis=0)
    queries = query[...]
    mixed = jnp.zeros(queries.shape, f32)
    logs = jnp.zeros(queries.shape, f32)
    for mask in lane_masks():
        own = queries * mask.astype(bf16)
        scores = jnp.where(allowed, nt(own, keys) * HEAD_DIM ** (-0.5), MASKED)
        maxima = jnp.max(scores, axis=1, keepdims=True)
        powered = jnp.exp(scores - maxima)
        totals = jnp.sum(powered, axis=1, keepdims=True)
        weights = (powered * (1.0 / totals)).astype(bf16)
        mixed = jnp.where(mask, nn(weights, values), mixed)
        logs = jnp.where(mask, maxima + jnp.log(totals), logs)
    mixture[...] = mixed.astype(bf16)
    logsum[...] = logs


def kernel_backward(
    causal,
    query,
    low_key,
    high_key,
    low_value,
    high_value,
    docs,
    blocks,
    ids,
    logsum,
    grad_mixture,
    grad_query,
    kept,
    sent,
):
    factor = HEAD_DIM ** (-0.5)
    allowed = allowed_of((docs, blocks), ids[...], causal)
    keys = jnp.concatenate([low_key[...], high_key[...]], axis=0)
    values = jnp.concatenate([low_value[...], high_value[...]], axis=0)
    queries = query[...]
    grads = grad_mixture[...]
    grad_queries = jnp.zeros(queries.shape, f32)
    grad_keys = jnp.zeros(keys.shape, f32)
    grad_values = jnp.zeros(keys.shape, f32)
    for head, mask in enumerate(lane_masks()):
        own = queries * mask.astype(bf16)
        own_grads = grads * mask.astype(bf16)
        scores = jnp.where(allowed, nt(own, keys) * factor, MASKED)
        low = HEAD_DIM * head
        probs = jnp.exp(scores - logsum[:, low:low + 1])
        grad_probs = nt(own_grads, values)
        deltas = jnp.sum(probs * grad_probs, axis=1, keepdims=True)
        grad_scores = (probs * (grad_probs - deltas)).astype(bf16)
        grad_queries = jnp.where(mask, nn(grad_scores, keys) * factor, grad_queries)
        grad_keys = grad_keys + tn(grad_scores, own) * factor
        grad_values = grad_values + tn(probs.astype(bf16), own_grads)
    grad_query[...] = grad_queries.astype(bf16)
    shape = (kept.shape[0], kept.shape[2], LANES)
    middle = keys.shape[0] // 2
    kept[:, 0] = grad_keys[:middle].reshape(shape)
    kept[:, 1] = grad_values[:middle].reshape(shape)
    sent[:, 0] = grad_keys[middle:].reshape(shape).astype(bf16)
    sent[:, 1] = grad_values[middle:].reshape(shape).astype(bf16)


def attend_specs(rows, half, keys):
    steps = half // LANES
    column = pl.BlockSpec((rows, LANES), lambda h: (0, h))
    key = pl.BlockSpec((keys // 2, LANES), lambda h: (0, h))
    value = pl.BlockSpec((keys // 2, LANES), lambda h: (0, steps + h))
    identity = pl.BlockSpec((rows, 1), lambda h: (0, 0))
    both = pl.BlockSpec((2, keys), lambda h: (0, 0))
    return column, [column, key, key, value, value, identity, identity, both]


def attend_forward(queries, pairs, ids, causal):
    rows, half = queries.shape
    keys = 2 * pairs[0].shape[0]
    column, specs = attend_specs(rows, half, keys)
    elements = rows * keys * half
    return pl.pallas_call(
        lambda *refs: kernel_forward(causal, *refs),
        grid=(half // LANES,),
        in_specs=specs,
        out_specs=[column, column],
        out_shape=[
            jax.ShapeDtypeStruct((rows, half), bf16),
            jax.ShapeDtypeStruct((rows, half), f32),
        ],
        cost_estimate=pl.CostEstimate(
            flops=4 * elements,
            transcendentals=elements // HEAD_DIM,
            bytes_accessed=4 * half * (keys + 2 * rows),
        ),
        name="attend_forward",
    )(queries, pairs[0], pairs[1], pairs[0], pairs[1], *ids)


def attend_backward(queries, pairs, ids, causal, logsum, grad_mixture):
    rows, half = queries.shape
    keys = 2 * pairs[0].shape[0]
    column, specs = attend_specs(rows, half, keys)
    parts = keys // rows // 2
    grads = pl.BlockSpec((parts, 2, rows, LANES), lambda h: (0, 0, 0, h))
    elements = rows * keys * half
    return pl.pallas_call(
        lambda *refs: kernel_backward(causal, *refs),
        grid=(half // LANES,),
        in_specs=specs + [column, column],
        out_specs=[column, grads, grads],
        out_shape=[
            jax.ShapeDtypeStruct((rows, half), bf16),
            jax.ShapeDtypeStruct((parts, 2, rows, half), f32),
            jax.ShapeDtypeStruct((parts, 2, rows, half), bf16),
        ],
        cost_estimate=pl.CostEstimate(
            flops=10 * elements,
            transcendentals=elements // HEAD_DIM,
            bytes_accessed=8 * half * (keys + 2 * rows),
        ),
        name="attend_backward",
    )(queries, pairs[0], pairs[1], pairs[0], pairs[1], *ids, logsum, grad_mixture)


def project_pairs(summed_keys, summed_values, bias):
    return jnp.concatenate(
        [summed_keys.astype(bf16), (summed_values + bias.astype(f32)).astype(bf16)], axis=1
    )


def attention_grads(grad_queries, grad_pairs, source, memory):
    half = grad_queries.shape[1]
    flat_pairs = jnp.concatenate([grad_pairs[0], grad_pairs[1]], axis=1)
    joined = jnp.concatenate([grad_queries, flat_pairs], axis=1)
    parts = []
    for low in (0, half):
        if source is memory:
            part = tn(joined, source[:, low:low + half]).astype(bf16).reshape(3, half, half)
        else:
            part = jnp.concatenate(
                [
                    tn(grad_queries, source[:, low:low + half]).astype(bf16)[None],
                    tn(flat_pairs, memory[:, low:low + half])
                    .astype(bf16)
                    .reshape(2, half, half),
                ],
                axis=0,
            )
        parts.append(part)
    grad_qv = jnp.stack(
        [
            jnp.sum(grad_queries.astype(f32), axis=0),
            jnp.sum(grad_pairs[1].astype(f32), axis=0),
        ]
    )
    return joined, jnp.stack(parts, axis=1), grad_qv


def column_sum(array):
    return jnp.sum(array.astype(f32), axis=0)


def per_device(
    enc_input,
    dec_input,
    doc_ids,
    block_ids,
    enc_qkv_weight,
    enc_qv_bias,
    enc_out_weight,
    enc_out_bias,
    enc_up_weight,
    enc_up_bias,
    enc_down_weight,
    enc_down_bias,
    enc_norm_gain,
    enc_norm_bias,
    self_qkv_weight,
    self_qv_bias,
    self_out_weight,
    self_out_bias,
    cross_qkv_weight,
    cross_qv_bias,
    cross_out_weight,
    cross_out_bias,
    dec_up_weight,
    dec_up_bias,
    dec_down_weight,
    dec_down_bias,
    dec_norm_gain,
    dec_norm_bias,
    enc_cotangent,
    dec_cotangent,
):
    rows = enc_input.shape[0]
    sequence = doc_ids.shape[1]
    group = sequence // rows
    device = lax.axis_index("gy")
    offset = device % group * rows
    docs_row = lax.dynamic_index_in_dim(doc_ids, device // group, 0, keepdims=False)
    blocks_row = lax.dynamic_index_in_dim(block_ids, device // group, 0, keepdims=False)
    query_docs = lax.dynamic_slice_in_dim(docs_row, offset, rows)
    query_blocks = lax.dynamic_slice_in_dim(blocks_row, offset, rows)
    ids = (
        query_docs[:, None],
        query_blocks[:, None],
        jnp.stack(
            [group_order(docs_row, group, rows), group_order(blocks_row, group, rows)]
        ),
    )

    half = enc_input.shape[1]
    enc_fetch = Task(attention_fetch(enc_qkv_weight, enc_out_weight))
    self_fetch = Task(attention_fetch(self_qkv_weight, self_out_weight))
    cross_fetch = Task(attention_fetch(cross_qkv_weight, cross_out_weight))
    enc_fetch.advance(enc_fetch.pending)

    first = gx_first()
    units = enc_up_bias.shape[0] // 2
    vector_rows = jnp.concatenate(
        [
            enc_out_bias[None],
            enc_down_bias[None],
            self_out_bias[None],
            cross_out_bias[None],
            dec_down_bias[None],
            enc_norm_gain,
            enc_norm_bias,
            dec_norm_gain,
            dec_norm_bias,
            jnp.zeros((1, half), bf16),
        ],
        axis=0,
    )
    shards = [enc_up_weight.T, enc_down_weight, dec_up_weight.T, dec_down_weight]
    kept = [jnp.where(first, shard[:units], shard[units:]) for shard in shards]
    sent = [jnp.where(first, shard[units:], shard[:units]) for shard in shards]
    packed = jnp.concatenate([enc_input, dec_input, vector_rows] + sent, axis=0)
    other = gx_swap(packed)
    low = 0
    joined_parts = []
    for own in [enc_input, dec_input, vector_rows] + kept:
        part = other[low:low + own.shape[0]]
        joined_parts.append(trade_keep(own, part, 1))
        low += own.shape[0]
    enc_low, dec_low, vectors = joined_parts[:3]
    vectors = vectors.astype(f32)
    enc_gain, enc_shift = vectors[5:7], vectors[7:9]
    dec_gain, dec_shift = vectors[9:12], vectors[12:15]
    up_biases = [
        jnp.where(first, bias[:units], bias[units:]) for bias in (enc_up_bias, dec_up_bias)
    ]

    def widen(part, bias):
        lanes = lax.broadcasted_iota(jnp.int32, (units, LANES), 1)
        return jnp.concatenate([part, jnp.where(lanes == 0, bias[:, None], 0)], axis=1)

    enc_feed_fetch = Task(
        feed_fetch(jnp.stack([widen(joined_parts[3], up_biases[0]), widen(joined_parts[4], up_biases[0])]))
    )
    dec_feed_fetch = Task(
        feed_fetch(jnp.stack([widen(joined_parts[5], up_biases[1]), widen(joined_parts[6], up_biases[1])]))
    )
    cotangent_task = Task(join_chain(jnp.stack([enc_cotangent, dec_cotangent]), 2))

    enc_fetch.advance(enc_fetch.pending)
    for step in range(len(masks_down(lax.axis_size("gy"))) - 3):
        enc_fetch.advance(enc_fetch.pending)
    launch(enc_fetch.pending, self_fetch, cross_fetch)
    enc_fetch.advance(enc_fetch.pending)
    arrived = enc_fetch.pending
    enc_fetch.advance(arrived)
    launch(arrived, self_fetch)
    launch(enc_fetch.pending, self_fetch, enc_feed_fetch)

    enc_fetch.advance(enc_fetch.pending)
    enc_wide, enc_out_full = enc_fetch.result
    summed = nt(enc_low, enc_wide)
    enc_queries = (summed[:, :half] + enc_qv_bias[0].astype(f32)).astype(bf16)
    pairs = project_pairs(summed[:, half:2 * half], summed[:, 2 * half:], enc_qv_bias[1])
    enc_pairs = gather_group(pairs, group)
    enc_pairs = tick(enc_pairs, self_fetch, enc_feed_fetch, cross_fetch)
    enc_mix, enc_logsum = attend_forward(enc_queries, enc_pairs, ids, False)
    enc_mix = tick(enc_mix, self_fetch, enc_feed_fetch, cross_fetch, dec_feed_fetch)
    branch = gx_sum(nt(enc_mix, enc_out_full)) + vectors[0]
    x1, x1_norm = norm_forward(enc_low.astype(f32) + branch, enc_gain[0], enc_shift[0])
    x1_low = tick(x1.astype(bf16), self_fetch, enc_feed_fetch, cross_fetch, dec_feed_fetch)

    self_wide, self_out_full = self_fetch.finish()
    summed = nt(dec_low, self_wide)
    self_queries = (summed[:, :half] + self_qv_bias[0].astype(f32)).astype(bf16)
    pairs = project_pairs(summed[:, half:2 * half], summed[:, 2 * half:], self_qv_bias[1])
    self_pairs = gather_group(pairs, group)
    launch(self_pairs, cotangent_task)
    self_pairs = tick(self_pairs, enc_feed_fetch, cross_fetch, dec_feed_fetch)

    enc_weights = enc_feed_fetch.finish()
    enc_branch, enc_pres, enc_hiddens = hidden_forward(x1_low, enc_weights, 0)
    enc_branch = enc_branch + vectors[1]

    self_mix, self_logsum = attend_forward(self_queries, self_pairs, ids, True)
    self_mix = tick(self_mix, cross_fetch, dec_feed_fetch)
    self_branch = gx_sum(nt(self_mix, self_out_full)) + vectors[2]

    x2, x2_norm = norm_forward(x1 + enc_branch, enc_gain[1], enc_shift[1])
    memory = launch(x2.astype(bf16), cross_fetch, dec_feed_fetch)

    cross_wide, cross_out_full = cross_fetch.finish()
    summed = nt(memory, cross_wide[half:])
    pairs = project_pairs(summed[:, :half], summed[:, half:], cross_qv_bias[1])
    cross_pairs = gather_group(pairs, group)
    y1, y1_norm = norm_forward(dec_low.astype(f32) + self_branch, dec_gain[0], dec_shift[0])
    y1_low = y1.astype(bf16)
    cross_queries = (nt(y1_low, cross_wide[:half]) + cross_qv_bias[0].astype(f32)).astype(bf16)
    cross_mix, cross_logsum = attend_forward(cross_queries, cross_pairs, ids, False)
    launch(cross_mix, dec_feed_fetch)
    branch = gx_sum(nt(cross_mix, cross_out_full)) + vectors[3]
    y2, y2_norm = norm_forward(y1 + branch, dec_gain[1], dec_shift[1])
    y2_low = y2.astype(bf16)

    dec_weights = dec_feed_fetch.finish()
    branch, dec_pres, dec_hiddens = hidden_forward(y2_low, dec_weights, 0)
    y3, y3_norm = norm_forward(y2 + branch + vectors[4], dec_gain[2], dec_shift[2])

    cotangents = cotangent_task.finish().astype(f32)
    g3, gain_d2, shift_d2 = norm_backward(cotangents[1], y3_norm, dec_gain[2])
    g3_low = g3.astype(bf16)
    dec_grad_pres, grad = hidden_backward(g3_low, dec_weights, dec_pres)
    dec_feed = Task(
        feed_return(*hidden_grads(dec_grad_pres, dec_hiddens, y2_low, g3_low))
    )
    dec_feed.advance(dec_feed.pending)
    g2, gain_d1, shift_d1 = norm_backward(g3 + grad, y2_norm, dec_gain[1])

    g2_low = g2.astype(bf16)
    grad_mix = nn(g2_low, cross_out_full).astype(bf16)
    grad_queries, kept, sent = attend_backward(
        cross_queries, cross_pairs, ids, False, cross_logsum, grad_mix
    )
    cross_out_grads = tn(g2_low, cross_mix).astype(bf16)
    grad_pairs = tick(reduce_group(kept, sent, group), dec_feed)
    flat_pairs = jnp.concatenate([grad_pairs[0], grad_pairs[1]], axis=1)
    grad_memory = gx_sum(nn(flat_pairs, cross_wide[half:]))
    grad = gx_sum(nn(grad_queries, cross_wide[:half]))
    _, grad_wide, cross_qv_grads = attention_grads(grad_queries, grad_pairs, y1_low, memory)
    cross_task = Task(attention_return(grad_wide, cross_out_grads))
    e2, gain_e1, shift_e1 = norm_backward(cotangents[0] + grad_memory, x2_norm, enc_gain[1])
    g1, gain_d0, shift_d0 = norm_backward(g2 + grad, y1_norm, dec_gain[0])

    e2_low = launch(e2.astype(bf16), cross_task)
    enc_grad_pres, grad_e = hidden_backward(e2_low, enc_weights, enc_pres)
    enc_feed = Task(feed_return(*hidden_grads(enc_grad_pres, enc_hiddens, x1_low, e2_low)))

    g1_low = tick(g1.astype(bf16), dec_feed, cross_task, enc_feed)
    grad_mix = nn(g1_low, self_out_full).astype(bf16)
    self_grad_queries, kept, sent = attend_backward(
        self_queries, self_pairs, ids, True, self_logsum, grad_mix
    )
    self_out_grads = tn(g1_low, self_mix).astype(bf16)
    sent = tick(sent, dec_feed)
    self_grad_pairs = reduce_group(kept, sent, group)

    e1, gain_e0, shift_e0 = norm_backward(e2 + grad_e, x1_norm, enc_gain[0])
    e1_low = tick(e1.astype(bf16), dec_feed, cross_task, enc_feed)
    grad_mix = nn(e1_low, enc_out_full).astype(bf16)
    enc_grad_queries, kept, sent = attend_backward(
        enc_queries, enc_pairs, ids, False, enc_logsum, grad_mix
    )
    enc_out_grads = tn(e1_low, enc_mix).astype(bf16)
    sent = tick(sent, dec_feed, cross_task)
    enc_grad_pairs = reduce_group(kept, sent, group)

    launch(self_grad_pairs, enc_feed)
    joined, grad_wide, self_qv_grads = attention_grads(
        self_grad_queries, self_grad_pairs, dec_low, dec_low
    )
    self_grad = gx_sum(nn(joined, self_wide))
    self_task = Task(attention_return(grad_wide, self_out_grads, True))
    launch(enc_grad_pairs, cross_task, self_task)
    joined, grad_wide, enc_qv_grads = attention_grads(
        enc_grad_queries, enc_grad_pairs, enc_low, enc_low
    )
    enc_grad = gx_sum(nn(joined, enc_wide))
    enc_task = Task(attention_return(grad_wide, enc_out_grads))

    def rows_of(grad_pres):
        return jnp.concatenate([column_sum(part) for part in grad_pres]).reshape(-1, half)

    sums_task = Task(
        sum_chain(
            jnp.concatenate(
                [
                    jnp.stack([gain_e0, gain_e1, shift_e0, shift_e1]),
                    jnp.stack([gain_d0, gain_d1, gain_d2, shift_d0, shift_d1, shift_d2]),
                    gx_half(
                        jnp.stack(
                            [
                                column_sum(e1_low),
                                column_sum(e2_low),
                                column_sum(g1_low),
                                column_sum(g2_low),
                                column_sum(g3_low),
                            ]
                        )
                    ),
                    enc_qv_grads,
                    self_qv_grads,
                    cross_qv_grads,
                    true_order(
                        rows_of(enc_grad_pres).reshape(lax.axis_size('gy'), -1)
                    ).reshape(-1, half),
                    true_order(
                        rows_of(dec_grad_pres).reshape(lax.axis_size('gy'), -1)
                    ).reshape(-1, half),
                ],
                axis=0,
            ),
            enc_up_bias.shape[0] // 2,
        ),
    )
    enc_task.advance(enc_task.pending)
    tail = [dec_feed, cross_task, enc_feed, self_task, enc_task, sums_task]
    while any(task.pending is not None for task in tail):
        live = [task for task in tail if task.pending is not None]
        tick(e1_low, *live)
    dec_input_grad = gx_half(g1 + self_grad)
    enc_input_grad = gx_half(e1 + enc_grad)
    enc_large, self_large, cross_large = enc_task.result, self_task.result, cross_task.result
    enc_feed_large, dec_feed_large = enc_feed.result, dec_feed.result
    sums, up_sums = sums_task.result
    return (
        gx_half(memory),
        gx_half(y3.astype(bf16)),
        enc_input_grad,
        dec_input_grad,
        enc_large[0],
        sums[15:17],
        enc_large[1],
        sums[10],
        enc_feed_large[0],
        up_sums[0],
        enc_feed_large[1],
        sums[11],
        sums[0:2],
        sums[2:4],
        self_large[0],
        sums[17:19],
        self_large[1],
        sums[12],
        cross_large[0],
        sums[19:21],
        cross_large[1],
        sums[13],
        dec_feed_large[0],
        up_sums[1],
        dec_feed_large[1],
        sums[14],
        sums[4:7],
        sums[7:10],
    )


def solution(mesh):
    return jax.shard_map(
        per_device,
        mesh=mesh,
        in_specs=(
            P("gy", "gx"),
            P("gy", "gx"),
            P(),
            P(),
            P(None, "gx", "gy"),
            P(None, "gx"),
            P("gx", "gy"),
            P("gx"),
            P("gx", "gy"),
            P("gy"),
            P("gy", "gx"),
            P("gx"),
            P(None, "gx"),
            P(None, "gx"),
            P(None, "gx", "gy"),
            P(None, "gx"),
            P("gx", "gy"),
            P("gx"),
            P(None, "gx", "gy"),
            P(None, "gx"),
            P("gx", "gy"),
            P("gx"),
            P("gx", "gy"),
            P("gy"),
            P("gy", "gx"),
            P("gx"),
            P(None, "gx"),
            P(None, "gx"),
            P("gy", "gx"),
            P("gy", "gx"),
        ),
        out_specs=(
            P("gy", "gx"),
            P("gy", "gx"),
            P("gy", "gx"),
            P("gy", "gx"),
            P(None, "gx", "gy"),
            P(None, "gx"),
            P("gx", "gy"),
            P("gx"),
            P("gx", "gy"),
            P("gy"),
            P("gy", "gx"),
            P("gx"),
            P(None, "gx"),
            P(None, "gx"),
            P(None, "gx", "gy"),
            P(None, "gx"),
            P("gx", "gy"),
            P("gx"),
            P(None, "gx", "gy"),
            P(None, "gx"),
            P("gx", "gy"),
            P("gx"),
            P("gx", "gy"),
            P("gy"),
            P("gy", "gx"),
            P("gx"),
            P(None, "gx"),
            P(None, "gx"),
        ),
        check_vma=False,
    )
```
